32 devices in a mesh: dp: 8 (over z, core), seq: 4 (over y, x).
Axes of the slice: x: 2, y: 2, z: 4, core: 2. Of those that a mesh axis runs over, the one named last changes fastest.
Arguments:
- queries: bfloat16 [8, 512, 4096], P('dp', 'seq'), may hold values from -6 to 6
- keys: bfloat16 [8, 512, 4096], P('dp', 'seq'), may hold values from -6 to 6
- values: bfloat16 [8, 512, 4096], P('dp', 'seq'), may hold values from -6 to 6
- cotangent: bfloat16 [8, 512, 4096], P('dp', 'seq'), may hold values from -6 to 6
- query_gain: float32 [32, 128], replicated, may hold values from 0.1 to 1.9
- key_gain: float32 [32, 128], replicated, may hold values from 0.1 to 1.9
- block_ids: int32 [8, 8], replicated, may hold values from -1 to 7, as said below
Outputs:
- out: bfloat16 [8, 512, 4096], P('dp', 'seq')
- query_grad: bfloat16 [8, 512, 4096], P('dp', 'seq')
- key_grad: bfloat16 [8, 512, 4096], P('dp', 'seq')
- value_grad: bfloat16 [8, 512, 4096], P('dp', 'seq')
- query_gain_grad: float32 [32, 128], replicated
- key_gain_grad: float32 [32, 128], replicated
The draws below stay inside these ranges and needn't reach their ends.
Inputs may be any that keep to these rules, and one draw needn't show every extreme that they name: `block_ids`: every row block r lists block r, block 0 and block 7, two window slots for blocks r - 1 and r + 1 (set to -1 where such a block is missing or is block 0 or 7), and three further blocks; no block is listed twice in a row.
All inputs are finite; a program needn't handle non-finite values.
Results may differ from the reference program's by a relative error of at most 0.011.
Values may be sent and summed in bfloat16 or wider, within the bound.
A program may use at most 128 MiB of HBM per device.

```python
import jax
import jax.numpy as jnp
from jax import lax

HEADS = 32
HEAD = 128
BLOCK = 64
SEQ_LEN = 512
NB = 8
BATCH = 8


def draw_block_ids(key, part):
    rows = jnp.arange(NB, dtype=jnp.int32)
    last = NB - 1
    window = jnp.stack([rows - 1, rows, rows + 1], axis=1)
    window = jnp.where((window <= 0) | (window >= last), -1, window)
    global_pair = jnp.stack([jnp.zeros_like(rows), jnp.full_like(rows, last)], axis=1)
    columns = jnp.arange(NB, dtype=jnp.int32)
    nearby = jnp.abs(columns[None, :] - rows[:, None]) <= 1
    taken = nearby | (columns[None, :] == 0) | (columns[None, :] == last)
    random_part = jax.random.randint(key, (NB, NB), 0, 1 << 20, dtype=jnp.int32)
    ranking = jnp.where(taken, (1 << 30) + columns[None, :], random_part * NB + columns[None, :])
    picked = jnp.argsort(ranking, axis=1)[:, :3].astype(jnp.int32)
    return jnp.concatenate([window, global_pair, picked], axis=1).astype(jnp.int32)


def shard_levels(own_key, shape, pieces, smallest, largest):
    def one(axis_at, shards_of):
        heights = jax.random.uniform(jax.random.fold_in(jax.random.fold_in(own_key, 6), axis_at), (shards_of,), jnp.float32, smallest / len(pieces), largest / len(pieces))
        return jnp.repeat(jnp.exp(heights), shape[axis_at] // shards_of).reshape((-1,) + (1,) * (len(shape) - axis_at - 1))

    factor_of = one(*pieces[0])
    for cut in pieces[1:]:
        factor_of = factor_of * one(*cut)
    return factor_of


def normal_values(stream_key, shape, spread, limit, cuts=(), held_as=jnp.bfloat16):
    values = spread * jax.random.normal(stream_key, shape, jnp.float32)
    if cuts:
        values = values * shard_levels(stream_key, shape, cuts, -0.22, 0.18)
    return jnp.clip(values, -limit, limit).astype(held_as)


def setup_inputs(seed: int = 0) -> dict:
    arg_keys = jax.random.split(jax.random.key(seed), 8)
    queries = normal_values(arg_keys[0], (BATCH, SEQ_LEN, HEADS * HEAD), 1.0, 6.0, ((0, 8), (1, 4)))
    keys = normal_values(arg_keys[1], (BATCH, SEQ_LEN, HEADS * HEAD), 1.0, 6.0, ((0, 8), (1, 4)))
    values = normal_values(arg_keys[2], (BATCH, SEQ_LEN, HEADS * HEAD), 1.0, 6.0, ((0, 8), (1, 4)))
    cotangent = normal_values(arg_keys[3], (BATCH, SEQ_LEN, HEADS * HEAD), 1.0, 6.0, ((0, 8), (1, 4)))
    query_gain = jnp.clip(1.0 + 0.18 * jax.random.normal(arg_keys[4], (HEADS, HEAD), jnp.float32), 0.1, 1.9)
    key_gain = jnp.clip(1.0 + 0.18 * jax.random.normal(arg_keys[5], (HEADS, HEAD), jnp.float32), 0.1, 1.9)
    block_ids = draw_block_ids(jax.random.fold_in(arg_keys[7], 71), 0)
    return dict(queries=queries, keys=keys, values=values, cotangent=cotangent, query_gain=query_gain, key_gain=key_gain, block_ids=block_ids)


EPSILON = 1e-06

def stored(array):
    return lax.optimization_barrier(array.astype(jnp.bfloat16))

def normalize(values, gain):
    inverse = lax.rsqrt(lax.optimization_barrier(jnp.mean(values * values, axis=-1, keepdims=True)) + EPSILON)
    return values * inverse * gain

def gather_blocks(array, safe_ids):
    count, length, heads, depth = array.shape
    blocks = array.reshape(count, length // BLOCK, BLOCK, heads, depth)
    picked = blocks[:, safe_ids]
    return picked.reshape(count, length // BLOCK, safe_ids.shape[1] * BLOCK, heads, depth).astype(jnp.float32)

def probabilities(query_rows, keys_near, valid_wide):
    depth = query_rows.shape[-1]
    scores = jnp.einsum('brqhd,brshd->bhrqs', query_rows.astype(jnp.float32), keys_near) * depth ** (-0.5)
    raised = jnp.where(valid_wide[None, None, :, None, :], jnp.exp(scores), 0.0)
    return raised / lax.optimization_barrier(jnp.sum(raised, axis=4, keepdims=True))

def attend_backward(query, keys, values, cotangent, ids):
    count, length, heads, depth = query.shape
    nblocks = length // BLOCK
    valid = ids >= 0
    safe_ids = jnp.maximum(ids, 0).astype(jnp.int32)
    valid_wide = jnp.repeat(valid, BLOCK, axis=1)
    keys_near = gather_blocks(keys, safe_ids)
    values_near = gather_blocks(values, safe_ids)
    query_rows = query.reshape(count, nblocks, BLOCK, heads, depth).astype(jnp.float32)
    probs = probabilities(query_rows, keys_near, valid_wide)
    weights = stored(probs).astype(jnp.float32)
    mixed = jnp.einsum('bhrqs,brshd->brqhd', weights, values_near)
    output = stored(mixed.reshape(query.shape))
    grad_rows = cotangent.reshape(count, nblocks, BLOCK, heads, depth).astype(jnp.float32)
    delta = lax.optimization_barrier(jnp.sum(cotangent.astype(jnp.float32) * output.astype(jnp.float32), axis=-1))
    delta = jnp.transpose(delta.reshape(count, nblocks, BLOCK, heads), (0, 3, 1, 2))
    grad_weights = jnp.einsum('brqhd,brshd->bhrqs', grad_rows, values_near)
    grad_scores = stored(probs * (grad_weights - delta[..., None]) * depth ** (-0.5)).astype(jnp.float32)
    grad_query = jnp.einsum('bhrqs,brshd->brqhd', grad_scores, keys_near)
    grad_query = stored(grad_query.reshape(query.shape))
    key_terms = jnp.einsum('bhrqs,brqhd->rsbhd', grad_scores, query_rows)
    value_terms = jnp.einsum('bhrqs,brqhd->rsbhd', weights, grad_rows)
    targets = jnp.where(valid, ids, nblocks).reshape(-1).astype(jnp.int32)

    def collect(terms):
        flat = terms.reshape((nblocks * ids.shape[1], BLOCK) + terms.shape[2:])
        summed = jax.ops.segment_sum(flat, targets, num_segments=nblocks)
        return stored(jnp.transpose(summed, (2, 0, 1, 3, 4)).reshape(query.shape))
    return (output, grad_query, collect(key_terms), collect(value_terms))

def reference(queries, keys, values, cotangent, query_gain, key_gain, block_ids):

    def one_sequence(items):
        query_seq, key_seq, value_seq, grad_seq = items
        shape_heads = (1, SEQ_LEN, HEADS, HEAD)
        query_raw = query_seq.reshape(shape_heads).astype(jnp.float32)
        key_raw = key_seq.reshape(shape_heads).astype(jnp.float32)
        query_norm = stored(normalize(query_raw, query_gain))
        key_norm = stored(normalize(key_raw, key_gain))
        value_heads = value_seq.reshape(shape_heads)
        grad_heads = grad_seq.reshape(shape_heads)
        output, grad_qn, grad_kn, grad_value = attend_backward(query_norm, key_norm, value_heads, grad_heads, block_ids)
        _, pull_query = jax.vjp(normalize, query_raw, query_gain)
        query_back, query_gain_back = pull_query(grad_qn.astype(jnp.float32))
        _, pull_key = jax.vjp(normalize, key_raw, key_gain)
        key_back, key_gain_back = pull_key(grad_kn.astype(jnp.float32))
        flat = (SEQ_LEN, HEADS * HEAD)
        return (output.reshape(flat), query_back.astype(jnp.bfloat16).reshape(flat), key_back.astype(jnp.bfloat16).reshape(flat), grad_value.reshape(flat), query_gain_back, key_gain_back)
    results = lax.map(one_sequence, (queries, keys, values, cotangent))
    factor = (BATCH * SEQ_LEN) ** (-0.5)
    return (results[0], results[1], results[2], results[3], lax.optimization_barrier(jnp.sum(results[4], axis=0)) * factor, lax.optimization_barrier(jnp.sum(results[5], axis=0)) * factor)
```

```python
import functools

import jax
import jax.numpy as jnp
from jax import lax
from jax.experimental import pallas as pl
from jax.experimental.pallas import tpu as pltpu
from jax.sharding import PartitionSpec as P

BLOCK = 64
EPSILON = 1e-06
MESH = pl.DeviceIdType.MESH
F32 = jnp.float32
BF16 = jnp.bfloat16


def peer_of(me, step, n):
    if n & (n - 1):
        return lax.rem(me + step, n)
    other, bit = me, 1
    while bit < n:
        if step & bit:
            other = other + bit - 2 * bit * ((me // bit) % 2)
        bit *= 2
    return other


def dot(a, b, contract):
    return lax.dot_general(a, b, ((contract[:1], contract[1:]), ((), ())), preferred_element_type=F32)


def kernel(
    n, m, factor,
    q_in, k_in, v_in, g_in, q_gain, k_gain, ids,
    o_out, q_out, k_out, v_out, gains_out,
    held, made, mask, k_norm, k_sum, v_sum, part, slots, total,
    in_send, in_recv, out_send, out_recv, part_send, part_recv, gain_send, gain_recv,
):
    seq, dp = lax.axis_index("seq"), lax.axis_index("dp")
    count, tokens, width = q_in.shape
    units, _, length, depth = held.shape
    heads = units // count
    rows = min(length, max(BLOCK, 131072 // length))
    scale = depth ** (-0.5)
    ins, outs = (q_in, k_in, v_in, g_in), (o_out, q_out, k_out, v_out)

    barrier = pltpu.get_barrier_semaphore()
    for step in range(1, n):
        pl.semaphore_signal(barrier, inc=1, device_id={"seq": peer_of(seq, step, n)}, device_id_type=MESH)
    for step in range(1, m):
        pl.semaphore_signal(barrier, inc=1, device_id={"dp": peer_of(dp, step, m)}, device_id_type=MESH)

    column_block = lax.broadcasted_iota(jnp.int32, (BLOCK, length), 1) // BLOCK

    def mask_row(r, carry):
        found = column_block == ids[r, 0]
        for j in range(1, ids.shape[1]):
            found = found | (column_block == ids[r, j])
        mask[pl.ds(pl.multiple_of(r * BLOCK, BLOCK), BLOCK), :] = jnp.where(found, 1.0, 0.0)
        return carry

    part[...] = jnp.zeros_like(part)
    pl.semaphore_wait(barrier, n + m - 2)

    def columns(owner, hl):
        return pl.ds(pl.multiple_of((owner * heads + hl) * depth, depth), depth)

    def token_rows(owner):
        return pl.ds(pl.multiple_of(owner * tokens, tokens), tokens)

    def send_in(u, carry):
        c, hl = u // heads, u % heads
        for t in range(4):
            for step in range(1, n):
                peer = peer_of(seq, step, n)
                pltpu.make_async_remote_copy(
                    src_ref=ins[t].at[c, :, columns(peer, hl)],
                    dst_ref=held.at[u, t, token_rows(seq), :],
                    send_sem=in_send.at[t],
                    recv_sem=in_recv.at[u],
                    device_id={"seq": peer},
                    device_id_type=MESH,
                ).start()
            pltpu.make_async_copy(
                ins[t].at[c, :, columns(seq, hl)],
                held.at[u, t, token_rows(seq), :],
                in_recv.at[u],
            ).start()
        return carry

    lax.fori_loop(0, units, send_in, 0)
    lax.fori_loop(0, ids.shape[0], mask_row, 0)

    def normed(raw):
        inverse = lax.rsqrt(jnp.mean(raw * raw, axis=-1, keepdims=True) + EPSILON)
        return raw * inverse, inverse

    def raw_grad(grad, gain, hat, inverse):
        scaled = grad * gain
        return inverse * (scaled - hat * jnp.mean(scaled * hat, axis=-1, keepdims=True))

    def one_head(u, carry):
        c, hl = u // heads, u % heads
        pltpu.make_async_copy(held.at[u], held.at[u], in_recv.at[u]).wait()
        gain_row = pl.ds(seq * heads + hl, 1)
        gain_q, gain_k = q_gain[gain_row, :], k_gain[gain_row, :]
        k_hat, _ = normed(held[u, 1].astype(F32))
        k_norm[...] = (k_hat * gain_k).astype(BF16)
        k_sum[...] = jnp.zeros_like(k_sum)
        v_sum[...] = jnp.zeros_like(v_sum)

        def some_rows(i, gain_sum):
            at = pl.ds(pl.multiple_of(i * rows, rows), rows)
            q_hat, q_inverse = normed(held[u, 0, at, :].astype(F32))
            q_norm = (q_hat * gain_q).astype(BF16)
            grad = held[u, 3, at, :]
            scores = dot(q_norm, k_norm[...], (1, 1)) * scale
            raised = jnp.exp(scores) * mask[at, :]
            probs = raised * (1.0 / jnp.sum(raised, axis=-1, keepdims=True))
            weights = probs.astype(BF16)
            out = dot(weights, held[u, 2], (1, 0)).astype(BF16)
            made[u, 0, at, :] = out
            delta = jnp.sum(grad.astype(F32) * out.astype(F32), axis=-1, keepdims=True)
            grad_probs = dot(grad, held[u, 2], (1, 1))
            grad_scores = (probs * (grad_probs - delta)).astype(BF16)
            grad_qn = (dot(grad_scores, k_norm[...], (1, 0)) * scale).astype(BF16).astype(F32)
            made[u, 1, at, :] = raw_grad(grad_qn, gain_q, q_hat, q_inverse).astype(BF16)
            v_sum[...] += dot(weights, grad, (0, 0))
            k_sum[...] += dot(grad_scores, q_norm, (0, 0))
            return gain_sum + jnp.sum(grad_qn * q_hat, axis=0, keepdims=True)

        gain_sum = lax.fori_loop(0, length // rows, some_rows, jnp.zeros((1, depth), F32))
        grad_kn = (k_sum[...] * scale).astype(BF16).astype(F32)
        k_hat, k_inverse = normed(held[u, 1].astype(F32))
        made[u, 2] = raw_grad(grad_kn, gain_k, k_hat, k_inverse).astype(BF16)
        made[u, 3] = v_sum[...].astype(BF16)
        here = pl.ds(hl, 1)
        part[0, here, :] += gain_sum
        part[1, here, :] += jnp.sum(grad_kn * k_hat, axis=0, keepdims=True)
        for t in range(4):
            for step in range(1, n):
                peer = peer_of(seq, step, n)
                pltpu.make_async_remote_copy(
                    src_ref=made.at[u, t, token_rows(peer), :],
                    dst_ref=outs[t].at[c, :, columns(seq, hl)],
                    send_sem=out_send.at[t],
                    recv_sem=out_recv.at[t],
                    device_id={"seq": peer},
                    device_id_type=MESH,
                ).start()
            pltpu.make_async_copy(
                made.at[u, t, token_rows(seq), :],
                outs[t].at[c, :, columns(seq, hl)],
                out_recv.at[t],
            ).start()
        return carry

    lax.fori_loop(0, units, one_head, 0)

    for step in range(1, m):
        pltpu.make_async_remote_copy(
            src_ref=part,
            dst_ref=slots.at[dp],
            send_sem=part_send,
            recv_sem=part_recv,
            device_id={"dp": peer_of(dp, step, m)},
            device_id_type=MESH,
        ).start()
    pltpu.make_async_copy(part, slots.at[dp], part_recv).start()
    pltpu.make_async_copy(slots, slots, part_recv).wait()
    summed = slots[0]
    for j in range(1, m):
        summed = summed + slots[j]
    total[...] = summed * factor
    for step in range(1, n):
        pltpu.make_async_remote_copy(
            src_ref=total,
            dst_ref=gains_out.at[seq],
            send_sem=gain_send,
            recv_sem=gain_recv,
            device_id={"seq": peer_of(seq, step, n)},
            device_id_type=MESH,
        ).start()
    pltpu.make_async_copy(total, gains_out.at[seq], gain_recv).start()

    sent = pl.ds(0, (n - 1) * heads * depth)
    for t in range(4):
        away = ins[t].at[:, :, sent]
        pltpu.make_async_copy(away, away, in_send.at[t]).wait()
    for t in range(4):
        away = made.at[:, t, pl.ds(0, (n - 1) * tokens), :]
        pltpu.make_async_copy(away, away, out_send.at[t]).wait()
    others = slots.at[pl.ds(0, m - 1)]
    pltpu.make_async_copy(others, others, part_send).wait()
    others = gains_out.at[pl.ds(0, n - 1)]
    pltpu.make_async_copy(others, others, gain_send).wait()
    for t in range(4):
        pltpu.make_async_copy(outs[t], outs[t], out_recv.at[t]).wait()
    pltpu.make_async_copy(gains_out, gains_out, gain_recv).wait()


def on_device(n, m, queries, keys, values, cotangent, query_gain, key_gain, block_ids):
    count, tokens, width = queries.shape
    all_heads, depth = query_gain.shape
    heads, length = all_heads // n, tokens * n
    units = count * heads
    factor = (count * m * length) ** (-0.5)
    any_space = pl.BlockSpec(memory_space=pl.ANY)
    vmem = pl.BlockSpec(memory_space=pltpu.VMEM)
    block = jax.ShapeDtypeStruct(queries.shape, BF16)
    out, query_grad, key_grad, value_grad, gains = pl.pallas_call(
        functools.partial(kernel, n, m, factor),
        out_shape=(block,) * 4 + (jax.ShapeDtypeStruct((n, 2, heads, depth), F32),),
        in_specs=[any_space] * 4 + [vmem] * 2 + [pl.BlockSpec(memory_space=pltpu.SMEM)],
        out_specs=(any_space,) * 4 + (vmem,),
        scratch_shapes=[
            pltpu.VMEM((units, 4, length, depth), BF16),
            pltpu.VMEM((units, 4, length, depth), BF16),
            pltpu.VMEM((length, length), F32),
            pltpu.VMEM((length, depth), BF16),
            pltpu.VMEM((length, depth), F32),
            pltpu.VMEM((length, depth), F32),
            pltpu.VMEM((2, heads, depth), F32),
            pltpu.VMEM((m, 2, heads, depth), F32),
            pltpu.VMEM((2, heads, depth), F32),
            pltpu.SemaphoreType.DMA((4,)),
            pltpu.SemaphoreType.DMA((units,)),
            pltpu.SemaphoreType.DMA((4,)),
            pltpu.SemaphoreType.DMA((4,)),
            pltpu.SemaphoreType.DMA,
            pltpu.SemaphoreType.DMA,
            pltpu.SemaphoreType.DMA,
            pltpu.SemaphoreType.DMA,
        ],
        compiler_params=pltpu.CompilerParams(
            collective_id=0, has_side_effects=True, vmem_limit_bytes=60 * 1024 * 1024
        ),
        name="attention",
    )(queries, keys, values, cotangent, query_gain, key_gain, block_ids)
    return (
        out, query_grad, key_grad, value_grad,
        gains[:, 0].reshape(all_heads, depth),
        gains[:, 1].reshape(all_heads, depth),
    )


def solution(mesh):
    sharded, copied = P("dp", "seq", None), P()
    return jax.shard_map(
        functools.partial(on_device, mesh.shape["seq"], mesh.shape["dp"]),
        mesh=mesh,
        in_specs=(sharded,) * 4 + (copied,) * 3,
        out_specs=(sharded,) * 4 + (copied,) * 2,
        check_vma=False,
    )
```

```python
import functools

import jax
import jax.numpy as jnp
from jax import lax
from jax.experimental import pallas as pl
from jax.experimental.pallas import tpu as pltpu
from jax.sharding import PartitionSpec as P

BLOCK = 64
EPSILON = 1e-06
VMEM_BYTES = 67043328
MESH = pl.DeviceIdType.MESH
F32 = jnp.float32
BF16 = jnp.bfloat16


def peer_of(me, step, n):
    if n & (n - 1):
        return lax.rem(me + step, n)
    other, bit = me, 1
    while bit < n:
        if step & bit:
            other = other + bit - 2 * bit * ((me // bit) % 2)
        bit *= 2
    return other


def dot(a, b, contract):
    return lax.dot_general(a, b, ((contract[:1], contract[1:]), ((), ())), preferred_element_type=F32)


def kernel(
    n, m, factor,
    q_in, k_in, v_in, g_in, q_gain_in, k_gain_in, ids_in,
    o_out, q_out, k_out, v_out, gains_out,
    held, made, mask, k_norm, k_sum, v_sum, part, slots, total,
    q_gain, k_gain, ids, in_send, in_recv, out_send, out_recv, part_send, part_recv, gain_send, gain_recv, small,
):
    seq, dp = lax.axis_index("seq"), lax.axis_index("dp")
    count, tokens, width = q_in.shape
    units, _, length, depth = held.shape
    heads = units // count
    rows = min(length, max(BLOCK, 131072 // length))
    scale = depth ** (-0.5)
    ins, outs = (q_in, k_in, v_in, g_in), (o_out, q_out, k_out, v_out)

    barrier = pltpu.get_barrier_semaphore()
    for step in range(1, n):
        pl.semaphore_signal(barrier, inc=1, device_id={"seq": peer_of(seq, step, n)}, device_id_type=MESH)
    for step in range(1, m):
        pl.semaphore_signal(barrier, inc=1, device_id={"dp": peer_of(dp, step, m)}, device_id_type=MESH)

    small_copies = [
        pltpu.make_async_copy(source, target, small.at[i])
        for i, (source, target) in enumerate(((q_gain_in, q_gain), (k_gain_in, k_gain), (ids_in, ids)))
    ]
    for copy in small_copies:
        copy.start()
    column_block = lax.broadcasted_iota(jnp.int32, (BLOCK, length), 1) // BLOCK

    def mask_row(r, carry):
        found = column_block == ids[r, 0]
        for j in range(1, ids.shape[1]):
            found = found | (column_block == ids[r, j])
        mask[pl.ds(pl.multiple_of(r * BLOCK, BLOCK), BLOCK), :] = jnp.where(found, 1.0, 0.0)
        return carry

    part[...] = jnp.zeros_like(part)
    pl.semaphore_wait(barrier, n + m - 2)

    def columns(owner, hl):
        return pl.ds(pl.multiple_of((owner * heads + hl) * depth, depth), depth)

    def token_rows(owner):
        return pl.ds(pl.multiple_of(owner * tokens, tokens), tokens)

    def send_in(u, carry):
        c, hl = u // heads, u % heads
        for t in range(4):
            for step in range(1, n):
                peer = peer_of(seq, step, n)
                pltpu.make_async_remote_copy(
                    src_ref=ins[t].at[c, :, columns(peer, hl)],
                    dst_ref=held.at[u, t, token_rows(seq), :],
                    send_sem=in_send.at[t],
                    recv_sem=in_recv.at[u],
                    device_id={"seq": peer},
                    device_id_type=MESH,
                ).start()
            pltpu.make_async_copy(
                ins[t].at[c, :, columns(seq, hl)],
                held.at[u, t, token_rows(seq), :],
                in_recv.at[u],
            ).start()
        return carry

    lax.fori_loop(0, units, send_in, 0)
    for copy in small_copies:
        copy.wait()
    lax.fori_loop(0, ids.shape[0], mask_row, 0)

    def normed(raw):
        inverse = lax.rsqrt(jnp.mean(raw * raw, axis=-1, keepdims=True) + EPSILON)
        return raw * inverse, inverse

    def raw_grad(grad, gain, hat, inverse):
        scaled = grad * gain
        return inverse * (scaled - hat * jnp.mean(scaled * hat, axis=-1, keepdims=True))

    def one_head(u, carry):
        c, hl = u // heads, u % heads
        pltpu.make_async_copy(held.at[u], held.at[u], in_recv.at[u]).wait()
        gain_row = pl.ds(seq * heads + hl, 1)
        gain_q, gain_k = q_gain[gain_row, :], k_gain[gain_row, :]
        k_hat, _ = normed(held[u, 1].astype(F32))
        k_norm[...] = (k_hat * gain_k).astype(BF16)
        k_sum[...] = jnp.zeros_like(k_sum)
        v_sum[...] = jnp.zeros_like(v_sum)

        def some_rows(i, gain_sum):
            at = pl.ds(pl.multiple_of(i * rows, rows), rows)
            q_hat, q_inverse = normed(held[u, 0, at, :].astype(F32))
            q_norm = (q_hat * gain_q).astype(BF16)
            grad = held[u, 3, at, :]
            scores = dot(q_norm, k_norm[...], (1, 1)) * scale
            raised = jnp.exp(scores) * mask[at, :]
            probs = raised * (1.0 / jnp.sum(raised, axis=-1, keepdims=True))
            weights = probs.astype(BF16)
            out = dot(weights, held[u, 2], (1, 0)).astype(BF16)
            made[u, 0, at, :] = out
            delta = jnp.sum(grad.astype(F32) * out.astype(F32), axis=-1, keepdims=True)
            grad_probs = dot(grad, held[u, 2], (1, 1))
            grad_scores = (probs * (grad_probs - delta)).astype(BF16)
            grad_qn = (dot(grad_scores, k_norm[...], (1, 0)) * scale).astype(BF16).astype(F32)
            made[u, 1, at, :] = raw_grad(grad_qn, gain_q, q_hat, q_inverse).astype(BF16)
            v_sum[...] += dot(weights, grad, (0, 0))
            k_sum[...] += dot(grad_scores, q_norm, (0, 0))
            return gain_sum + jnp.sum(grad_qn * q_hat, axis=0, keepdims=True)

        gain_sum = lax.fori_loop(0, length // rows, some_rows, jnp.zeros((1, depth), F32))
        grad_kn = (k_sum[...] * scale).astype(BF16).astype(F32)
        k_hat, k_inverse = normed(held[u, 1].astype(F32))
        made[u, 2] = raw_grad(grad_kn, gain_k, k_hat, k_inverse).astype(BF16)
        made[u, 3] = v_sum[...].astype(BF16)
        here = pl.ds(hl, 1)
        part[0, here, :] += gain_sum
        part[1, here, :] += jnp.sum(grad_kn * k_hat, axis=0, keepdims=True)
        for t in range(4):
            for step in range(1, n):
                peer = peer_of(seq, step, n)
                pltpu.make_async_remote_copy(
                    src_ref=made.at[u, t, token_rows(peer), :],
                    dst_ref=outs[t].at[c, :, columns(seq, hl)],
                    send_sem=out_send.at[t],
                    recv_sem=out_recv.at[t],
                    device_id={"seq": peer},
                    device_id_type=MESH,
                ).start()
            pltpu.make_async_copy(
                made.at[u, t, token_rows(seq), :],
                outs[t].at[c, :, columns(seq, hl)],
                out_recv.at[t],
            ).start()
        return carry

    lax.fori_loop(0, units, one_head, 0)

    for step in range(1, m):
        pltpu.make_async_remote_copy(
            src_ref=part,
            dst_ref=slots.at[dp],
            send_sem=part_send,
            recv_sem=part_recv,
            device_id={"dp": peer_of(dp, step, m)},
            device_id_type=MESH,
        ).start()
    pltpu.make_async_copy(part, slots.at[dp], part_recv).start()
    pltpu.make_async_copy(slots, slots, part_recv).wait()
    summed = slots[0]
    for j in range(1, m):
        summed = summed + slots[j]
    total[...] = summed * factor
    for step in range(1, n):
        pltpu.make_async_remote_copy(
            src_ref=total,
            dst_ref=gains_out.at[seq],
            send_sem=gain_send,
            recv_sem=gain_recv,
            device_id={"seq": peer_of(seq, step, n)},
            device_id_type=MESH,
        ).start()
    pltpu.make_async_copy(total, gains_out.at[seq], gain_recv).start()

    sent = pl.ds(0, (n - 1) * heads * depth)
    for t in range(4):
        away = ins[t].at[:, :, sent]
        pltpu.make_async_copy(away, away, in_send.at[t]).wait()
    for t in range(4):
        away = made.at[:, t, pl.ds(0, (n - 1) * tokens), :]
        pltpu.make_async_copy(away, away, out_send.at[t]).wait()
    others = slots.at[pl.ds(0, m - 1)]
    pltpu.make_async_copy(others, others, part_send).wait()
    others = gains_out.at[pl.ds(0, n - 1)]
    pltpu.make_async_copy(others, others, gain_send).wait()
    for t in range(4):
        pltpu.make_async_copy(outs[t], outs[t], out_recv.at[t]).wait()
    pltpu.make_async_copy(gains_out, gains_out, gain_recv).wait()


def hand_over(o_in, q_in, k_in, v_in, gains_in, o_out, q_out, k_out, v_out, q_gain, k_gain, sems):
    copies = [
        pltpu.make_async_copy(source, target, sems.at[t])
        for t, (source, target) in enumerate(
            ((o_in, o_out), (q_in, q_out), (k_in, k_out), (v_in, v_out))
        )
    ]
    for copy in copies:
        copy.start()
    heads = gains_in.shape[2]
    for j in range(gains_in.shape[0]):
        q_gain[j * heads : (j + 1) * heads, :] = gains_in[j, 0]
        k_gain[j * heads : (j + 1) * heads, :] = gains_in[j, 1]
    for copy in copies:
        copy.wait()


def on_device(n, m, queries, keys, values, cotangent, query_gain, key_gain, block_ids):
    count, tokens, width = queries.shape
    all_heads, depth = query_gain.shape
    heads, length = all_heads // n, tokens * n
    units = count * heads
    factor = (count * m * length) ** (-0.5)
    hbm = pl.BlockSpec(memory_space=pltpu.HBM)
    vmem = pl.BlockSpec(memory_space=pltpu.VMEM)
    landing = pltpu.VMEM(queries.shape, BF16)
    landed = 4 * queries.size * 2 + 2 * query_gain.size * 4
    received = pl.pallas_call(
        functools.partial(kernel, n, m, factor),
        out_shape=(landing,) * 4 + (pltpu.VMEM((n, 2, heads, depth), F32),),
        in_specs=[hbm] * 7,
        out_specs=(vmem,) * 5,
        scratch_shapes=[
            pltpu.VMEM((units, 4, length, depth), BF16),
            pltpu.VMEM((units, 4, length, depth), BF16),
            pltpu.VMEM((length, length), F32),
            pltpu.VMEM((length, depth), BF16),
            pltpu.VMEM((length, depth), F32),
            pltpu.VMEM((length, depth), F32),
            pltpu.VMEM((2, heads, depth), F32),
            pltpu.VMEM((m, 2, heads, depth), F32),
            pltpu.VMEM((2, heads, depth), F32),
            pltpu.VMEM(query_gain.shape, F32),
            pltpu.VMEM(key_gain.shape, F32),
            pltpu.SMEM(block_ids.shape, jnp.int32),
            pltpu.SemaphoreType.DMA((4,)),
            pltpu.SemaphoreType.DMA((units,)),
            pltpu.SemaphoreType.DMA((4,)),
            pltpu.SemaphoreType.DMA((4,)),
            pltpu.SemaphoreType.DMA,
            pltpu.SemaphoreType.DMA,
            pltpu.SemaphoreType.DMA,
            pltpu.SemaphoreType.DMA,
            pltpu.SemaphoreType.DMA((3,)),
        ],
        compiler_params=pltpu.CompilerParams(
            collective_id=0, has_side_effects=True, vmem_limit_bytes=VMEM_BYTES - landed - 524288
        ),
        name="attention",
    )(queries, keys, values, cotangent, query_gain, key_gain, block_ids)
    block = jax.ShapeDtypeStruct(queries.shape, BF16)
    gain = jax.ShapeDtypeStruct(query_gain.shape, F32)
    return pl.pallas_call(
        hand_over,
        out_shape=(block,) * 4 + (gain,) * 2,
        in_specs=[vmem] * 5,
        out_specs=(hbm,) * 4 + (vmem,) * 2,
        scratch_shapes=[pltpu.SemaphoreType.DMA((4,))],
        compiler_params=pltpu.CompilerParams(vmem_limit_bytes=16 * 1024 * 1024),
        name="hand_over",
    )(*received)


def solution(mesh):
    sharded, copied = P("dp", "seq", None), P()
    return jax.shard_map(
        functools.partial(on_device, mesh.shape["seq"], mesh.shape["dp"]),
        mesh=mesh,
        in_specs=(sharded,) * 4 + (copied,) * 3,
        out_specs=(sharded,) * 4 + (copied,) * 2,
        check_vma=False,
    )
```

```python
import functools

import jax
import jax.numpy as jnp
from jax import lax
from jax.experimental import pallas as pl
from jax.experimental.pallas import tpu as pltpu
from jax.sharding import PartitionSpec as P

BLOCK = 64
EPSILON = 1e-06
VMEM_BYTES = 67043328
MESH = pl.DeviceIdType.MESH
F32 = jnp.float32
BF16 = jnp.bfloat16


def peer_of(me, step, n):
    if n & (n - 1):
        return lax.rem(me + step, n)
    other, bit = me, 1
    while bit < n:
        if step & bit:
            other = other + bit - 2 * bit * ((me // bit) % 2)
        bit *= 2
    return other


def dot(a, b, contract):
    return lax.dot_general(a, b, ((contract[:1], contract[1:]), ((), ())), preferred_element_type=F32)


def kernel(
    n, m, factor,
    q_in, k_in, v_in, g_in, q_gain_in, k_gain_in, ids_in,
    o_out, q_out, k_out, v_out, gains_out,
    held, made, mask, k_norm, k_sum, v_sum, part, slots, total,
    q_gain, k_gain, ids, in_send, in_recv, out_send, out_recv, part_send, part_recv, gain_send, gain_recv, small,
    ready, joined,
):
    seq, dp = lax.axis_index("seq"), lax.axis_index("dp")
    count, tokens, width = q_in.shape
    units, _, length, depth = held.shape
    heads = units // count
    rows = min(length, max(BLOCK, 131072 // length))
    scale = depth ** (-0.5)
    ins, outs = (q_in, k_in, v_in, g_in), (o_out, q_out, k_out, v_out)

    barrier = pltpu.get_barrier_semaphore()
    gate = seq == 0
    for step in range(1, n):
        peer = peer_of(seq, step, n)

        @pl.when(peer != 0)
        def _():
            pl.semaphore_signal(barrier, inc=1, device_id={"seq": peer}, device_id_type=MESH)

    small_copies = [
        pltpu.make_async_copy(source, target, small.at[i])
        for i, (source, target) in enumerate(((q_gain_in, q_gain), (k_gain_in, k_gain), (ids_in, ids)))
    ]
    for copy in small_copies:
        copy.start()
    column_block = lax.broadcasted_iota(jnp.int32, (BLOCK, length), 1) // BLOCK

    def mask_row(r, carry):
        found = column_block == ids[r, 0]
        for j in range(1, ids.shape[1]):
            found = found | (column_block == ids[r, j])
        mask[pl.ds(pl.multiple_of(r * BLOCK, BLOCK), BLOCK), :] = jnp.where(found, 1.0, 0.0)
        return carry

    part[...] = jnp.zeros_like(part)

    @pl.when(jnp.logical_not(gate))
    def _():
        pl.semaphore_wait(barrier, n - 1)
        pl.semaphore_signal(ready, inc=1, device_id={"seq": 0}, device_id_type=MESH)

    @pl.when(gate)
    def _():
        pl.semaphore_wait(ready, n - 1)
        for step in range(1, m):
            pl.semaphore_signal(barrier, inc=1, device_id={"dp": peer_of(dp, step, m)}, device_id_type=MESH)

    def columns(owner, hl):
        return pl.ds(pl.multiple_of((owner * heads + hl) * depth, depth), depth)

    def token_rows(owner):
        return pl.ds(pl.multiple_of(owner * tokens, tokens), tokens)

    def send_in(u, carry):
        c, hl = u // heads, u % heads
        for t in range(4):
            for step in range(1, n):
                peer = peer_of(seq, step, n)
                pltpu.make_async_remote_copy(
                    src_ref=ins[t].at[c, :, columns(peer, hl)],
                    dst_ref=held.at[u, t, token_rows(seq), :],
                    send_sem=in_send.at[t],
                    recv_sem=in_recv.at[u],
                    device_id={"seq": peer},
                    device_id_type=MESH,
                ).start()
            pltpu.make_async_copy(
                ins[t].at[c, :, columns(seq, hl)],
                held.at[u, t, token_rows(seq), :],
                in_recv.at[u],
            ).start()
        return carry

    lax.fori_loop(0, units, send_in, 0)
    for copy in small_copies:
        copy.wait()
    lax.fori_loop(0, ids.shape[0], mask_row, 0)

    def normed(raw):
        inverse = lax.rsqrt(jnp.mean(raw * raw, axis=-1, keepdims=True) + EPSILON)
        return raw * inverse, inverse

    def raw_grad(grad, gain, hat, inverse):
        scaled = grad * gain
        return inverse * (scaled - hat * jnp.mean(scaled * hat, axis=-1, keepdims=True))

    def one_head(u, carry):
        c, hl = u // heads, u % heads
        pltpu.make_async_copy(held.at[u], held.at[u], in_recv.at[u]).wait()
        gain_row = pl.ds(seq * heads + hl, 1)
        gain_q, gain_k = q_gain[gain_row, :], k_gain[gain_row, :]
        k_hat, _ = normed(held[u, 1].astype(F32))
        k_norm[...] = (k_hat * gain_k).astype(BF16)
        k_sum[...] = jnp.zeros_like(k_sum)
        v_sum[...] = jnp.zeros_like(v_sum)

        def some_rows(i, gain_sum):
            at = pl.ds(pl.multiple_of(i * rows, rows), rows)
            q_hat, q_inverse = normed(held[u, 0, at, :].astype(F32))
            q_norm = (q_hat * gain_q).astype(BF16)
            grad = held[u, 3, at, :]
            scores = dot(q_norm, k_norm[...], (1, 1)) * scale
            raised = jnp.exp(scores) * mask[at, :]
            probs = raised * (1.0 / jnp.sum(raised, axis=-1, keepdims=True))
            weights = probs.astype(BF16)
            out = dot(weights, held[u, 2], (1, 0)).astype(BF16)
            made[u, 0, at, :] = out
            delta = jnp.sum(grad.astype(F32) * out.astype(F32), axis=-1, keepdims=True)
            grad_probs = dot(grad, held[u, 2], (1, 1))
            grad_scores = (probs * (grad_probs - delta)).astype(BF16)
            grad_qn = (dot(grad_scores, k_norm[...], (1, 0)) * scale).astype(BF16).astype(F32)
            made[u, 1, at, :] = raw_grad(grad_qn, gain_q, q_hat, q_inverse).astype(BF16)
            v_sum[...] += dot(weights, grad, (0, 0))
            k_sum[...] += dot(grad_scores, q_norm, (0, 0))
            return gain_sum + jnp.sum(grad_qn * q_hat, axis=0, keepdims=True)

        gain_sum = lax.fori_loop(0, length // rows, some_rows, jnp.zeros((1, depth), F32))
        grad_kn = (k_sum[...] * scale).astype(BF16).astype(F32)
        k_hat, k_inverse = normed(held[u, 1].astype(F32))
        made[u, 2] = raw_grad(grad_kn, gain_k, k_hat, k_inverse).astype(BF16)
        made[u, 3] = v_sum[...].astype(BF16)
        here = pl.ds(hl, 1)
        part[0, here, :] += gain_sum
        part[1, here, :] += jnp.sum(grad_kn * k_hat, axis=0, keepdims=True)
        for t in range(4):
            for step in range(1, n):
                peer = peer_of(seq, step, n)
                pltpu.make_async_remote_copy(
                    src_ref=made.at[u, t, token_rows(peer), :],
                    dst_ref=outs[t].at[c, :, columns(seq, hl)],
                    send_sem=out_send.at[t],
                    recv_sem=out_recv.at[t],
                    device_id={"seq": peer},
                    device_id_type=MESH,
                ).start()
            pltpu.make_async_copy(
                made.at[u, t, token_rows(seq), :],
                outs[t].at[c, :, columns(seq, hl)],
                out_recv.at[t],
            ).start()
        return carry

    lax.fori_loop(0, units, one_head, 0)

    @pl.when(gate)
    def _():
        pl.semaphore_wait(barrier, m - 1)
        for step in range(1, n):
            pl.semaphore_signal(joined, inc=1, device_id={"seq": step}, device_id_type=MESH)

    @pl.when(jnp.logical_not(gate))
    def _():
        pl.semaphore_wait(joined, 1)

    for step in range(1, m):
        pltpu.make_async_remote_copy(
            src_ref=part,
            dst_ref=slots.at[dp],
            send_sem=part_send,
            recv_sem=part_recv,
            device_id={"dp": peer_of(dp, step, m)},
            device_id_type=MESH,
        ).start()
    pltpu.make_async_copy(part, slots.at[dp], part_recv).start()
    pltpu.make_async_copy(slots, slots, part_recv).wait()
    summed = slots[0]
    for j in range(1, m):
        summed = summed + slots[j]
    total[...] = summed * factor
    for step in range(1, n):
        pltpu.make_async_remote_copy(
            src_ref=total,
            dst_ref=gains_out.at[seq],
            send_sem=gain_send,
            recv_sem=gain_recv,
            device_id={"seq": peer_of(seq, step, n)},
            device_id_type=MESH,
        ).start()
    pltpu.make_async_copy(total, gains_out.at[seq], gain_recv).start()

    sent = pl.ds(0, (n - 1) * heads * depth)
    for t in range(4):
        away = ins[t].at[:, :, sent]
        pltpu.make_async_copy(away, away, in_send.at[t]).wait()
    for t in range(4):
        away = made.at[:, t, pl.ds(0, (n - 1) * tokens), :]
        pltpu.make_async_copy(away, away, out_send.at[t]).wait()
    others = slots.at[pl.ds(0, m - 1)]
    pltpu.make_async_copy(others, others, part_send).wait()
    others = gains_out.at[pl.ds(0, n - 1)]
    pltpu.make_async_copy(others, others, gain_send).wait()
    for t in range(4):
        pltpu.make_async_copy(outs[t], outs[t], out_recv.at[t]).wait()
    pltpu.make_async_copy(gains_out, gains_out, gain_recv).wait()


def hand_over(o_in, q_in, k_in, v_in, gains_in, o_out, q_out, k_out, v_out, q_gain, k_gain, sems):
    copies = [
        pltpu.make_async_copy(source, target, sems.at[t])
        for t, (source, target) in enumerate(
            ((o_in, o_out), (q_in, q_out), (k_in, k_out), (v_in, v_out))
        )
    ]
    for copy in copies:
        copy.start()
    heads = gains_in.shape[2]
    for j in range(gains_in.shape[0]):
        q_gain[j * heads : (j + 1) * heads, :] = gains_in[j, 0]
        k_gain[j * heads : (j + 1) * heads, :] = gains_in[j, 1]
    for copy in copies:
        copy.wait()


def on_device(n, m, queries, keys, values, cotangent, query_gain, key_gain, block_ids):
    count, tokens, width = queries.shape
    all_heads, depth = query_gain.shape
    heads, length = all_heads // n, tokens * n
    units = count * heads
    factor = (count * m * length) ** (-0.5)
    hbm = pl.BlockSpec(memory_space=pltpu.HBM)
    vmem = pl.BlockSpec(memory_space=pltpu.VMEM)
    landing = pltpu.VMEM(queries.shape, BF16)
    landed = 4 * queries.size * 2 + 2 * query_gain.size * 4
    received = pl.pallas_call(
        functools.partial(kernel, n, m, factor),
        out_shape=(landing,) * 4 + (pltpu.VMEM((n, 2, heads, depth), F32),),
        in_specs=[hbm] * 7,
        out_specs=(vmem,) * 5,
        scratch_shapes=[
            pltpu.VMEM((units, 4, length, depth), BF16),
            pltpu.VMEM((units, 4, length, depth), BF16),
            pltpu.VMEM((length, length), F32),
            pltpu.VMEM((length, depth), BF16),
            pltpu.VMEM((length, depth), F32),
            pltpu.VMEM((length, depth), F32),
            pltpu.VMEM((2, heads, depth), F32),
            pltpu.VMEM((m, 2, heads, depth), F32),
            pltpu.VMEM((2, heads, depth), F32),
            pltpu.VMEM(query_gain.shape, F32),
            pltpu.VMEM(key_gain.shape, F32),
            pltpu.SMEM(block_ids.shape, jnp.int32),
            pltpu.SemaphoreType.DMA((4,)),
            pltpu.SemaphoreType.DMA((units,)),
            pltpu.SemaphoreType.DMA((4,)),
            pltpu.SemaphoreType.DMA((4,)),
            pltpu.SemaphoreType.DMA,
            pltpu.SemaphoreType.DMA,
            pltpu.SemaphoreType.DMA,
            pltpu.SemaphoreType.DMA,
            pltpu.SemaphoreType.DMA((3,)),
            pltpu.SemaphoreType.REGULAR,
            pltpu.SemaphoreType.REGULAR,
        ],
        compiler_params=pltpu.CompilerParams(
            collective_id=0, has_side_effects=True, vmem_limit_bytes=VMEM_BYTES - landed - 524288
        ),
        name="attention",
    )(queries, keys, values, cotangent, query_gain, key_gain, block_ids)
    block = jax.ShapeDtypeStruct(queries.shape, BF16)
    gain = jax.ShapeDtypeStruct(query_gain.shape, F32)
    return pl.pallas_call(
        hand_over,
        out_shape=(block,) * 4 + (gain,) * 2,
        in_specs=[vmem] * 5,
        out_specs=(hbm,) * 4 + (vmem,) * 2,
        scratch_shapes=[pltpu.SemaphoreType.DMA((4,))],
        compiler_params=pltpu.CompilerParams(vmem_limit_bytes=16 * 1024 * 1024),
        name="hand_over",
    )(*received)


def solution(mesh):
    sharded, copied = P("dp", "seq", None), P()
    return jax.shard_map(
        functools.partial(on_device, mesh.shape["seq"], mesh.shape["dp"]),
        mesh=mesh,
        in_specs=(sharded,) * 4 + (copied,) * 3,
        out_specs=(sharded,) * 4 + (copied,) * 2,
        check_vma=False,
    )
```
